1024 devices in a mesh: blk: 16 (over x, y_lo), regroup: 16 (over z, core), hid: 4 (over y_hi).
Axes of the slice: x: 8, y: 8 (y_hi: 4, y_lo: 2; y = y_hi * 2 + y_lo), z: 8, core: 2. Of those that a mesh axis runs over, the one named last changes fastest.
Arguments:
- tokens: bfloat16 [4096, 6144], P(('blk', 'regroup')), may hold values from -6 to 6
- kinds: int32 [4096], P(('blk', 'regroup')), may hold values from 0 to 7
- slots: int32 [256, 16], P(('blk', 'regroup')), may hold values from 0 to 15, each once within a row
- gains: float32 [8, 6144], replicated, may hold values from 0.1 to 1.9
- gate_weight: bfloat16 [6144, 16384], P(None, ('blk', 'hid')), may hold values from -0.078125 to 0.078125
- up_weight: bfloat16 [6144, 16384], P(None, ('blk', 'hid')), may hold values from -0.078125 to 0.078125
- down_weight: bfloat16 [16384, 6144], P(('blk', 'hid')), may hold values from -0.125 to 0.125
Outputs:
- mixed: bfloat16 [4096, 6144], P(('blk', 'regroup'), 'hid')
The draws below stay inside these ranges and needn't reach their ends.
Inputs may be any that keep to these rules, and one draw needn't show every extreme that they name: Each row of slots names every number 0 to 15 once.
All inputs are finite; a program needn't handle non-finite values.
Results may differ from the reference program's by a relative error of at most 0.019.
Values may be sent and summed in bfloat16 or wider, within the bound.
A program may use at most 64 MiB of HBM per device.

```python
import jax
import jax.numpy as jnp
from jax import lax

D = 6144
FF = 16384
KINDS = 8
PAT_DEV = 16
BLOCKS = 16
LANES = 16
ROUNDS = 1
TOKENS = 4096
SHARDS = 64
SHARD_FF = 256


def plant(values, stream_key, smallest, high):
    shape = values.shape
    place = [jax.random.randint(jax.random.fold_in(stream_key, axis), (), 0, shape[axis]) for axis in range(len(shape))]
    values = values.at[tuple(place)].set(smallest)
    longest = shape.index(max(shape))
    place[longest] = (place[longest] + 1) % shape[longest]
    return values.at[tuple(place)].set(high)


def with_spikes(entries, rng, source, target, shards_of, factor):
    def block_of(dim):
        return (jnp.arange(entries.shape[dim]) // (entries.shape[dim] // shards_of)).reshape((-1,) + (1,) * (entries.ndim - 1 - dim))

    near = jax.random.permutation(rng, shards_of)[block_of(target)]
    far = (block_of(target) + shards_of // 2) % shards_of
    return jnp.where((block_of(source) == near) | (block_of(source) == far), factor * entries, entries)


def block_scale(own_key, extent, split, low, high):
    factor_of, own = 1.0, jax.random.fold_in(own_key, 6)
    for axis_at, shards_of in split:
        heights = jnp.exp(jax.random.uniform(jax.random.fold_in(own, axis_at), (shards_of,), jnp.float32, low / len(split), high / len(split)))
        factor_of = factor_of * jnp.repeat(heights, extent[axis_at] // shards_of).reshape([-1 if axis == axis_at else 1 for axis in range(len(extent))])
    return factor_of


def gaussian(own_key, shape, spread, bound, cuts=(), held_as=jnp.bfloat16):
    factor_of = block_scale(own_key, shape, cuts, -0.22, 0.18) if cuts else 1.0
    array = jax.random.normal(own_key, shape, jnp.float32) * spread * factor_of
    return jnp.minimum(jnp.maximum(array, -bound), bound).astype(held_as)


def bell_draw_with(own_key, dims, deviation, most, split, heavy, dtype=jnp.bfloat16):
    array = deviation * jax.random.normal(own_key, dims, jnp.float32)
    if split:
        array = array * block_scale(own_key, dims, split, -0.22, 0.18)
    return jnp.clip(with_spikes(array, jax.random.fold_in(own_key, 3), *heavy), -most, most).astype(dtype)


def setup_inputs(seed: int = 0) -> dict:
    key_of = jax.random.split(jax.random.key(seed), 8)
    return {
        "tokens": gaussian(key_of[0], (TOKENS, D), 1.0, 6.0, ((0, 256),)),
        "kinds": plant(jax.random.randint(key_of[1], (TOKENS,), 0, KINDS), jax.random.fold_in(key_of[1], 1), 0, KINDS - 1).astype(jnp.int32),
        "slots": jax.vmap(lambda own: jax.random.permutation(own, PAT_DEV))(jax.random.split(key_of[2], (BLOCKS * LANES))).reshape((BLOCKS * LANES, PAT_DEV)).astype(jnp.int32),
        "gains": jnp.clip(1.0 + 0.18 * jax.random.normal(key_of[3], (KINDS, D), jnp.float32), 0.1, 1.9),
        "gate_weight": gaussian(key_of[4], (D, FF), D ** -0.5, 0.078125, ((1, 64),)),
        "up_weight": gaussian(key_of[5], (D, FF), D ** -0.5, 0.078125, ((1, 64),)),
        "down_weight": bell_draw_with(key_of[6], (FF, D), FF ** -0.5, 0.125, ((0, 64),), (0, 1, 64, 4.0)),
    }


epsilon = 1e-05

def reference(tokens, kinds, slots, gains, gate_weight, up_weight, down_weight):
    width = tokens.shape[1]
    float_rows = tokens.astype(jnp.float32)
    row_scale = lax.rsqrt(lax.optimization_barrier(jnp.mean(float_rows * float_rows, axis=1, keepdims=True)) + epsilon)
    normed = (float_rows * row_scale * gains[kinds]).astype(jnp.bfloat16)
    grouped = normed.reshape(BLOCKS * LANES, PAT_DEV, width)
    inverse = jnp.argsort(slots, axis=1).astype(jnp.int32)
    ordered = jnp.take_along_axis(grouped, inverse[:, :, None], axis=1)
    arranged = ordered.reshape(BLOCKS, LANES, ROUNDS, LANES, width)
    arranged = jnp.transpose(arranged, (0, 3, 2, 1, 4)).reshape(TOKENS, width)
    gate_full = jnp.dot(arranged, gate_weight, preferred_element_type=jnp.float32)
    up_full = jnp.dot(arranged, up_weight, preferred_element_type=jnp.float32)
    hidden = (jax.nn.silu(gate_full) * up_full).astype(jnp.bfloat16)
    hidden_shards = jnp.transpose(hidden.reshape(TOKENS, SHARDS, SHARD_FF), (1, 0, 2))
    down_shards = down_weight.reshape(SHARDS, SHARD_FF, width)

    def add_term(summed, operands):
        rounded = jnp.dot(operands[0], operands[1], preferred_element_type=jnp.float32).astype(jnp.bfloat16)
        rounded = lax.optimization_barrier(rounded)
        return (summed + rounded.astype(jnp.float32), None)
    summed, unused = lax.scan(add_term, jnp.zeros((TOKENS, width), jnp.float32), (hidden_shards, down_shards))
    return summed.astype(jnp.bfloat16)
```

```python
import jax
import jax.numpy as jnp
from jax import lax
from jax.experimental import pallas as pl
from jax.experimental.pallas import tpu as pltpu
from jax.sharding import PartitionSpec as P

MESH = pl.DeviceIdType.MESH
epsilon = 1e-05
D = 6144
HALF = D // 2
EIGHTH = D // 8
UNITS = 256
SLOT = {0: 0, 1: 1, 7: 2, 2: 3, 6: 4, 3: 5, 5: 6, 4: 7}
AHEAD = {u: d for d, u in SLOT.items()}
KSTEP = 1536


def kernel(
    tokens_ref, kinds_ref, slots_ref, gains_ref, gate_hbm, up_hbm, down_hbm, out_ref,
    panel, wg, wu, wd, hid, acc_g, acc_u, part_f, part, arrived, outgo, final, rows,
    load_sem, xs, xr, ys, yr, ws, wr, zs, zr, cs, cr, hs, hr, ps, pr, fs, fr, own_sem,
):
    blk, reg, hidx = lax.axis_index("blk"), lax.axis_index("regroup"), lax.axis_index("hid")
    x, ylo = lax.div(blk, 2), lax.rem(blk, 2)
    y = hidx * 2 + ylo
    z, core = lax.div(reg, 2), lax.rem(reg, 2)

    def device(x_at, y_at, reg_at):
        return (x_at * 2 + lax.rem(y_at, 2), reg_at, lax.div(y_at, 2))

    def along_x(d):
        return device(lax.rem(x + d, 8), y, reg)

    def along_y(d):
        return device(x, lax.rem(y + d, 8), reg)

    def along_z(d):
        return device(x, y, lax.rem(z + d, 8) * 2 + core)

    partner = device(x, y, z * 2 + 1 - core)
    y_other = hidx * 2 + 1 - ylo

    def regroup_peer(swap, t):
        return device(x, y_other if swap else y, lax.rem(reg + t, 16))

    barrier = pltpu.get_barrier_semaphore()
    peers = [along_x(d) for d in range(1, 8)] + [along_y(d) for d in range(1, 8)]
    peers += [regroup_peer(swap, t) for swap in (0, 1) for t in range(1, 16)]
    for peer in peers:
        pl.semaphore_signal(barrier, inc=1, device_id=peer, device_id_type=MESH)

    loads = [
        pltpu.make_async_copy(gate_hbm, wg, load_sem.at[0]),
        pltpu.make_async_copy(up_hbm, wu, load_sem.at[1]),
        pltpu.make_async_copy(
            down_hbm.at[:, pl.ds(pl.multiple_of(y * EIGHTH, 128), EIGHTH)], wd.at[0], load_sem.at[2]
        ),
    ]
    for load in loads:
        load.start()

    slot_row = slots_ref[...]
    here = lax.broadcasted_iota(jnp.int32, (16, 16), 0) == jnp.broadcast_to(slot_row, (16, 16))
    placing = jnp.where(here, 1.0, 0.0).astype(jnp.bfloat16)
    kind = jnp.sum(
        jnp.where(here, jnp.broadcast_to(kinds_ref[...], (16, 16)).astype(jnp.float32), 0.0),
        axis=1, keepdims=True,
    )
    values = jnp.dot(placing, tokens_ref[...], preferred_element_type=jnp.float32)
    scale = lax.rsqrt(jnp.mean(values * values, axis=1, keepdims=True) + epsilon)
    gain = jnp.broadcast_to(gains_ref[0:1, :], (16, D))
    for k in range(1, 8):
        gain = jnp.where(kind == float(k), jnp.broadcast_to(gains_ref[k : k + 1, :], (16, D)), gain)
    panel[ylo, 0] = (values * scale * gain).astype(jnp.bfloat16)

    pl.semaphore_wait(barrier, len(peers))
    sends = []

    def push(source, target, send_sem, recv_sem, peer):
        copy = pltpu.make_async_remote_copy(
            src_ref=source, dst_ref=target, send_sem=send_sem, recv_sem=recv_sem,
            device_id=peer, device_id_type=MESH,
        )
        copy.start()
        sends.append(copy)

    def arrive(target, send_sem, recv_sem):
        pltpu.make_async_remote_copy(
            src_ref=target, dst_ref=target, send_sem=send_sem, recv_sem=recv_sem,
            device_id=partner, device_id_type=MESH,
        ).wait_recv()

    def half(lane, d, h):
        return panel.at[lane, SLOT[d % 8], :, pl.ds(h * HALF, HALF)]

    def x_send(step, direction, h):
        d = (-step if direction == 0 else step) % 8
        to = (d - 1 if direction == 0 else d + 1) % 8
        push(half(ylo, d, h), half(ylo, to, h), xs.at[direction, step, h], xr.at[direction, step, h],
             along_x(1 if direction == 0 else 7))

    def x_wait(step, direction, h):
        d = (-step - 1 if direction == 0 else step + 1) % 8
        arrive(half(ylo, d, h), xs.at[direction, step, h], xr.at[direction, step, h])

    def y_send(d, h):
        push(half(ylo, d, h), half(ylo, d, h), ys.at[SLOT[d], h], yr.at[SLOT[d], h],
             along_y(1 if h == 0 else 7))

    def y_wait(u):
        for h in (0, 1):
            arrive(half(1 - ylo, AHEAD[u], h), ys.at[u, h], yr.at[u, h])

    def x_step(step):
        if step < 3:
            for h in (0, 1):
                for direction in (0, 1):
                    x_wait(step, direction, h)
                    if step < 2 or h == direction:
                        x_send(step + 1, direction, h)
                for direction in (0, 1):
                    y_send((-step - 1 if direction == 0 else step + 1) % 8, h)
        else:
            for h in (0, 1):
                x_wait(3, h, h)
                y_send(4, h)

    def piece(q, lo=0, width=EIGHTH):
        return wd.at[pl.ds(1, 7), pl.ds(pl.multiple_of(q * 16, 16), 16), pl.ds(lo, width)]

    def z_at(d):
        return lax.rem(z + d + 8, 8) * 2 + core

    def z_send(step, direction):
        q = z_at(-step if direction == 0 else step)
        lo, width = (0, EIGHTH) if step < 3 else (direction * (EIGHTH // 2), EIGHTH // 2)
        push(piece(q, lo, width), piece(q, lo, width), zs.at[direction, step], zr.at[direction, step],
             along_z(1 if direction == 0 else 7))

    def core_send(d):
        push(piece(z_at(d)), piece(z_at(d)), cs.at[d % 8], cr.at[d % 8], partner)

    def z_step(step):
        for direction in (0, 1):
            q = z_at(-step - 1 if direction == 0 else step + 1)
            lo, width = (0, EIGHTH) if step < 3 else (direction * (EIGHTH // 2), EIGHTH // 2)
            arrive(piece(q, lo, width), zs.at[direction, step], zr.at[direction, step])
            if step < 3:
                z_send(step + 1, direction)
                core_send(-step - 1 if direction == 0 else step + 1)
        if step == 3:
            core_send(4)

    def core_wait():
        for d in range(8):
            q = lax.rem(z + d, 8) * 2 + 1 - core
            arrive(piece(q), cs.at[d], cr.at[d])

    def hidden_at(dy, group, lo=0, count=128):
        return hid.at[dy % 8, group, pl.ds(lo, count), :]

    def hidden_send(group, step, direction):
        dy = -step if direction == 0 else step
        lo, count = (0, 128) if step < 3 else (direction * 64, 64)
        push(hidden_at(dy, group, lo, count),
             hidden_at(dy - 1 if direction == 0 else dy + 1, group, lo, count),
             hs.at[group, direction, step], hr.at[group, direction, step],
             along_y(1 if direction == 0 else 7))

    def hidden_step(group, step):
        for direction in (0, 1):
            dy = -step - 1 if direction == 0 else step + 1
            lo, count = (0, 128) if step < 3 else (direction * 64, 64)
            arrive(hidden_at(dy, group, lo, count), hs.at[group, direction, step],
                   hr.at[group, direction, step])
            if step < 3:
                hidden_send(group, step + 1, direction)

    def gate_up(group):
        acc_g[...] = jnp.zeros_like(acc_g)
        acc_u[...] = jnp.zeros_like(acc_u)

        def one(k, carry):
            span = pl.ds(pl.multiple_of(k * KSTEP, KSTEP), KSTEP)
            block = panel[:, 4 * group : 4 * group + 4, :, span].reshape(128, KSTEP)
            acc_g[...] += jnp.dot(block, wg[span, :], preferred_element_type=jnp.float32)
            acc_u[...] += jnp.dot(block, wu[span, :], preferred_element_type=jnp.float32)
            return carry

        lax.fori_loop(0, D // KSTEP, one, 0)
        v = acc_g[...]
        hid[0, group] = (v / (1.0 + jnp.exp(-v)) * acc_u[...]).astype(jnp.bfloat16)
        for direction in (0, 1):
            hidden_send(group, 0, direction)

    def down(group, pieces, first):
        for dy in pieces:
            term = jnp.dot(hid[dy, group], wd[dy], preferred_element_type=jnp.float32)
            if first and dy == pieces[0]:
                part_f[group] = term
            else:
                part_f[group] += term

    def part_send(group):
        part[:, 4 * group : 4 * group + 4] = part_f[group].reshape(2, 4, 16, EIGHTH).astype(jnp.bfloat16)
        for u in reversed(range(4 * group, 4 * group + 4)):
            d = AHEAD[u]
            if d:
                push(part.at[:, u], arrived.at[d], ps.at[d], pr.at[d], along_x(d))

    for h in (0, 1):
        for direction in (0, 1):
            x_send(0, direction, h)
        y_send(0, h)
    for t in (4, 3, 5, 2, 6, 1, 7):
        y_to = lax.rem(y + t, 8)
        push(
            down_hbm.at[pl.ds(pl.multiple_of(reg * 16, 16), 16),
                        pl.ds(pl.multiple_of(y_to * EIGHTH, 128), EIGHTH)],
            wd.at[8 - t, pl.ds(pl.multiple_of(reg * 16, 16), 16), :],
            ws.at[8 - t], wr.at[8 - t], along_y(t),
        )
    x_step(0)
    x_step(1)
    for t in range(1, 8):
        arrive(wd.at[t, pl.ds(pl.multiple_of(reg * 16, 16), 16), :], ws.at[t], wr.at[t])
    z_send(0, 0)
    z_send(0, 1)
    core_send(0)
    x_step(2)
    z_step(0)
    loads[0].wait()
    loads[1].wait()
    for u in range(4):
        y_wait(u)
    gate_up(0)
    x_step(3)
    z_step(1)
    hidden_step(0, 0)
    for u in range(4, 8):
        y_wait(u)
    gate_up(1)
    z_step(2)
    hidden_step(0, 1)
    hidden_step(0, 2)
    z_step(3)
    hidden_step(1, 0)
    hidden_step(0, 3)
    loads[2].wait()
    core_wait()
    down(0, range(8), True)
    part_send(0)
    hidden_step(1, 1)
    down(1, (0, 1, 7), True)
    hidden_step(1, 2)
    down(1, (2, 6), False)
    hidden_step(1, 3)
    down(1, (3, 5, 4), False)
    part_send(1)

    for lane in (0, 1):
        rows[lane] = part_f[0, 64 * lane : 64 * lane + 16, :]
    for d in (1, 7, 2, 6, 3, 5, 4):
        arrive(arrived.at[d], ps.at[d], pr.at[d])
        rows[...] += arrived[d].astype(jnp.float32)
    for lane in (0, 1):
        for j in range(16):
            outgo[lane, j] = rows[lane, j : j + 1, :]
    own = pltpu.make_async_copy(outgo.at[ylo, reg], final.at[ylo, reg], own_sem)
    own.start()
    for swap in (0, 1):
        lane = 1 - ylo if swap else ylo
        for t in range(16):
            if swap or t:
                push(outgo.at[lane, lax.rem(reg + t, 16)], final.at[ylo, reg],
                     fs.at[swap, t], fr.at[swap, t], regroup_peer(swap, t))
    own.wait()
    for swap in (0, 1):
        lane = 1 - ylo if swap else ylo
        for t in range(16):
            if swap or t:
                arrive(final.at[lane, lax.rem(reg + 16 - t, 16)], fs.at[swap, t], fr.at[swap, t])
    for lane in (0, 1):
        for g in range(16):
            rows[lane, g : g + 1, :] = final[lane, g]
        out_ref[:, lane * EIGHTH : (lane + 1) * EIGHTH] = rows[lane].astype(jnp.bfloat16)
    for copy in sends:
        copy.wait_send()


def on_device(tokens, kinds, slots, gains, gate_weight, up_weight, down_weight):
    vmem = pl.BlockSpec(memory_space=pltpu.VMEM)
    hbm = pl.BlockSpec(memory_space=pl.ANY)
    bf16, f32, dma = jnp.bfloat16, jnp.float32, pltpu.SemaphoreType.DMA
    return pl.pallas_call(
        kernel,
        out_shape=jax.ShapeDtypeStruct((16, D // 4), bf16),
        in_specs=[vmem, vmem, vmem, vmem, hbm, hbm, hbm],
        out_specs=vmem,
        scratch_shapes=[
            pltpu.VMEM((2, 8, 16, D), bf16),
            pltpu.VMEM((D, UNITS), bf16),
            pltpu.VMEM((D, UNITS), bf16),
            pltpu.VMEM((8, UNITS, EIGHTH), bf16),
            pltpu.VMEM((8, 2, 128, UNITS), bf16),
            pltpu.VMEM((128, UNITS), f32),
            pltpu.VMEM((128, UNITS), f32),
            pltpu.VMEM((2, 128, EIGHTH), f32),
            pltpu.VMEM((2, 8, 16, EIGHTH), bf16),
            pltpu.VMEM((8, 2, 16, EIGHTH), bf16),
            pltpu.VMEM((2, 16, 1, EIGHTH), f32),
            pltpu.VMEM((2, 16, 1, EIGHTH), f32),
            pltpu.VMEM((2, 16, EIGHTH), f32),
            dma((3,)),
            dma((2, 4, 2)), dma((2, 4, 2)),
            dma((8, 2)), dma((8, 2)),
            dma((8,)), dma((8,)),
            dma((2, 4)), dma((2, 4)),
            dma((8,)), dma((8,)),
            dma((2, 2, 4)), dma((2, 2, 4)),
            dma((8,)), dma((8,)),
            dma((2, 16)), dma((2, 16)),
            dma(()),
        ],
        compiler_params=pltpu.CompilerParams(collective_id=0, has_side_effects=True),
    )(tokens, kinds.reshape(1, 16), slots, gains, gate_weight, up_weight, down_weight)


def solution(mesh):
    placed = (
        P(("blk", "regroup"), None),
        P(("blk", "regroup")),
        P(("blk", "regroup"), None),
        P(),
        P(None, ("blk", "hid")),
        P(None, ("blk", "hid")),
        P(("blk", "hid"), None),
    )
    return jax.shard_map(
        on_device,
        mesh=mesh,
        in_specs=placed,
        out_specs=P(("blk", "regroup"), "hid"),
        check_vma=False,
    )
```

```python
import jax
import jax.numpy as jnp
from jax import lax
from jax.experimental import pallas as pl
from jax.experimental.pallas import tpu as pltpu
from jax.sharding import PartitionSpec as P

MESH = pl.DeviceIdType.MESH
epsilon = 1e-05
D = 6144
HALF = D // 2
EIGHTH = D // 8
UNITS = 256
SLOT = {0: 0, 1: 1, 7: 2, 2: 3, 6: 4, 3: 5, 5: 6, 4: 7}
AHEAD = {u: d for d, u in SLOT.items()}
KSTEP = 1536
MID, MID_WIDTH = 2304, 1536
GROUPS = ((0, 4), (4, 6), (6, 8))


def rows_of(group):
    lo, hi = GROUPS[group]
    return 32 * lo, 32 * (hi - lo)


def kernel(
    tokens_hbm, kinds_hbm, slots_hbm, gains_hbm, gate_hbm, up_hbm, down_hbm, out_ref,
    tokens_ref, kinds_ref, slots_ref, gains_ref, panel, wg, wu, wd, hid, acc_g, acc_u, part_f, part, arrived, outgo, final, rows,
    load_sem, xs, xr, ms, mr, ys, yr, ws, wr, zs, zr, cs, cr, hs, hr, ps, pr, fs, fr, own_sem,
):
    blk, reg, hidx = lax.axis_index("blk"), lax.axis_index("regroup"), lax.axis_index("hid")
    x, ylo = lax.div(blk, 2), lax.rem(blk, 2)
    y = hidx * 2 + ylo
    z, core = lax.div(reg, 2), lax.rem(reg, 2)

    def device(x_at, y_at, reg_at):
        return (x_at * 2 + lax.rem(y_at, 2), reg_at, lax.div(y_at, 2))

    def along_x(d):
        return device(lax.rem(x + d, 8), y, reg)

    def along_y(d):
        return device(x, lax.rem(y + d, 8), reg)

    def along_z(d):
        return device(x, y, lax.rem(z + d, 8) * 2 + core)

    partner = device(x, y, z * 2 + 1 - core)
    y_other = hidx * 2 + 1 - ylo

    def regroup_peer(swap, t):
        return device(x, y_other if swap else y, lax.rem(reg + t, 16))

    inputs = [
        pltpu.make_async_copy(tokens_hbm, tokens_ref, load_sem.at[3]),
        pltpu.make_async_copy(gains_hbm, gains_ref, load_sem.at[4]),
        pltpu.make_async_copy(kinds_hbm, kinds_ref, load_sem.at[5]),
        pltpu.make_async_copy(slots_hbm, slots_ref, load_sem.at[6]),
    ]
    for copy in inputs:
        copy.start()

    barrier = pltpu.get_barrier_semaphore()
    peers = [along_y(d) for d in (4, 3, 5, 2, 6, 1, 7)] + [along_x(1), along_x(7)]
    peers += [along_z(1), along_z(7), partner]
    for peer in peers:
        pl.semaphore_signal(barrier, inc=1, device_id=peer, device_id_type=MESH)

    loads = [
        pltpu.make_async_copy(gate_hbm, wg, load_sem.at[0]),
        pltpu.make_async_copy(up_hbm, wu, load_sem.at[1]),
        pltpu.make_async_copy(
            down_hbm.at[:, pl.ds(pl.multiple_of(y * EIGHTH, 128), EIGHTH)], wd.at[0], load_sem.at[2]
        ),
    ]
    for load in loads:
        load.start()
    for copy in inputs:
        copy.wait()

    slot_row = slots_ref[...]
    here = lax.broadcasted_iota(jnp.int32, (16, 16), 0) == jnp.broadcast_to(slot_row, (16, 16))
    placing = jnp.where(here, 1.0, 0.0).astype(jnp.bfloat16)
    kind = jnp.sum(
        jnp.where(here, jnp.broadcast_to(kinds_ref[...], (16, 16)).astype(jnp.float32), 0.0),
        axis=1, keepdims=True,
    )
    values = jnp.dot(placing, tokens_ref[...], preferred_element_type=jnp.float32)
    scale = lax.rsqrt(jnp.mean(values * values, axis=1, keepdims=True) + epsilon)
    gain = jnp.broadcast_to(gains_ref[0:1, :], (16, D))
    for k in range(1, 8):
        gain = jnp.where(kind == float(k), jnp.broadcast_to(gains_ref[k : k + 1, :], (16, D)), gain)
    panel[ylo, 0] = (values * scale * gain).astype(jnp.bfloat16)

    pl.semaphore_wait(barrier, len(peers))
    sends = []

    def push(source, target, send_sem, recv_sem, peer):
        copy = pltpu.make_async_remote_copy(
            src_ref=source, dst_ref=target, send_sem=send_sem, recv_sem=recv_sem,
            device_id=peer, device_id_type=MESH,
        )
        copy.start()
        sends.append(copy)

    def arrive(target, send_sem, recv_sem):
        pltpu.make_async_remote_copy(
            src_ref=target, dst_ref=target, send_sem=send_sem, recv_sem=recv_sem,
            device_id=partner, device_id_type=MESH,
        ).wait_recv()

    def half(lane, d, h):
        return panel.at[lane, SLOT[d % 8], :, pl.ds(h * HALF, HALF)]

    def x_send(step, direction, h):
        d = (-step if direction == 0 else step) % 8
        to = (d - 1 if direction == 0 else d + 1) % 8
        push(half(ylo, d, h), half(ylo, to, h), xs.at[direction, step, h], xr.at[direction, step, h],
             along_x(1 if direction == 0 else 7))

    def x_wait(step, direction, h):
        d = (-step - 1 if direction == 0 else step + 1) % 8
        arrive(half(ylo, d, h), xs.at[direction, step, h], xr.at[direction, step, h])

    def y_part(lane, d, h):
        if d == 0:
            return half(lane, d, h)
        lo, width = (0, MID) if h == 0 else (MID + MID_WIDTH, D - MID - MID_WIDTH)
        return panel.at[lane, SLOT[d], :, pl.ds(lo, width)]

    def y_send(d, h):
        push(y_part(ylo, d, h), y_part(ylo, d, h), ys.at[SLOT[d], h], yr.at[SLOT[d], h],
             along_y(1 if h == 0 else 7))

    def y_wait(u):
        for h in (0, 1):
            arrive(y_part(1 - ylo, AHEAD[u], h), ys.at[u, h], yr.at[u, h])

    def mid(d, step, direction):
        lo, width = (MID, MID_WIDTH) if step < 3 else (MID + direction * (MID_WIDTH // 2), MID_WIDTH // 2)
        return panel.at[1 - ylo, SLOT[d % 8], :, pl.ds(lo, width)]

    def mid_send(step, direction):
        d = -step if direction == 0 else step
        to = d - 1 if direction == 0 else d + 1
        push(mid(d, step, direction), mid(to, step, direction), ms.at[direction, step],
             mr.at[direction, step], along_x(1 if direction == 0 else 7))

    def mid_step(step):
        for direction in (0, 1):
            d = -step - 1 if direction == 0 else step + 1
            arrive(mid(d, step, direction), ms.at[direction, step], mr.at[direction, step])
            if step < 3:
                mid_send(step + 1, direction)

    def x_step(step, h):
        if step < 3:
            for direction in (0, 1):
                x_wait(step, direction, h)
                if step < 2 or h == direction:
                    x_send(step + 1, direction, h)
            for direction in (0, 1):
                y_send((-step - 1 if direction == 0 else step + 1) % 8, h)
        else:
            x_wait(3, h, h)
            y_send(4, h)

    def piece(q, part):
        return wd.at[pl.ds(1, 7), pl.ds(pl.multiple_of(q * 16, 16), 16), pl.ds(part * (EIGHTH // 2), EIGHTH // 2)]

    def z_at(d):
        return lax.rem(z + d + 8, 8) * 2 + core

    def z_send(step, direction, part):
        q = z_at(-step if direction == 0 else step)
        push(piece(q, part), piece(q, part), zs.at[direction, step, part], zr.at[direction, step, part],
             along_z(1 if direction == 0 else 7))

    def core_send(d, part):
        push(piece(z_at(d), part), piece(z_at(d), part), cs.at[d % 8, part], cr.at[d % 8, part], partner)

    def z_start():
        for part in (0, 1):
            for direction in (0, 1):
                z_send(0, direction, part)
        for part in (0, 1):
            core_send(0, part)

    def z_step(step, part):
        for direction in (0, 1) if step < 3 else (part,):
            d = -step - 1 if direction == 0 else step + 1
            arrive(piece(z_at(d), part), zs.at[direction, step, part], zr.at[direction, step, part])
            if step < 2 or (step == 2 and direction == part):
                z_send(step + 1, direction, part)
            core_send(4 if step == 3 else d, part)

    def core_wait():
        for d in range(8):
            q = lax.rem(z + d, 8) * 2 + 1 - core
            for part in (0, 1):
                arrive(piece(q, part), cs.at[d, part], cr.at[d, part])

    def hidden_at(dy, group, step, direction):
        start, count = rows_of(group)
        if step == 3:
            start, count = start + direction * (count // 2), count // 2
        return hid.at[dy % 8, pl.ds(start, count), :]

    def hidden_send(group, step, direction):
        dy = -step if direction == 0 else step
        push(hidden_at(dy, group, step, direction),
             hidden_at(dy - 1 if direction == 0 else dy + 1, group, step, direction),
             hs.at[group, direction, step], hr.at[group, direction, step],
             along_y(1 if direction == 0 else 7))

    def hidden_step(group, step):
        for direction in (0, 1):
            dy = -step - 1 if direction == 0 else step + 1
            arrive(hidden_at(dy, group, step, direction), hs.at[group, direction, step],
                   hr.at[group, direction, step])
            if step < 3:
                hidden_send(group, step + 1, direction)

    def gate_up(group):
        (lo, hi), (start, count) = GROUPS[group], rows_of(group)
        acc_g[0:count, :] = jnp.zeros((count, UNITS), jnp.float32)
        acc_u[0:count, :] = jnp.zeros((count, UNITS), jnp.float32)

        def one(k, carry):
            span = pl.ds(pl.multiple_of(k * KSTEP, KSTEP), KSTEP)
            block = panel[:, lo:hi, :, span].reshape(count, KSTEP)
            acc_g[0:count, :] += jnp.dot(block, wg[span, :], preferred_element_type=jnp.float32)
            acc_u[0:count, :] += jnp.dot(block, wu[span, :], preferred_element_type=jnp.float32)
            return carry

        lax.fori_loop(0, D // KSTEP, one, 0)
        v = acc_g[0:count, :]
        hid[0, start : start + count, :] = (v / (1.0 + jnp.exp(-v)) * acc_u[0:count, :]).astype(jnp.bfloat16)
        for direction in (0, 1):
            hidden_send(group, 0, direction)

    def down(group, pieces, first):
        start, count = rows_of(group)
        for dy in pieces:
            term = jnp.dot(hid[dy, start : start + count, :], wd[dy], preferred_element_type=jnp.float32)
            if first and dy == pieces[0]:
                part_f[start : start + count, :] = term
            else:
                part_f[start : start + count, :] += term

    def part_send(group):
        (lo, hi), (start, count) = GROUPS[group], rows_of(group)
        part[:, lo:hi] = part_f[start : start + count, :].reshape(2, hi - lo, 16, EIGHTH).astype(jnp.bfloat16)
        for u in reversed(range(lo, hi)):
            d = AHEAD[u]
            if d:
                push(part.at[:, u], arrived.at[d], ps.at[d], pr.at[d], along_x(d))

    def weights_wait():
        for t in range(1, 8):
            arrive(wd.at[t, pl.ds(pl.multiple_of(reg * 16, 16), 16), :], ws.at[t], wr.at[t])

    def y_waits(lo, hi):
        for u in range(lo, hi):
            y_wait(u)

    for h in (0, 1):
        for direction in (0, 1):
            x_send(0, direction, h)
        y_send(0, h)
    for t in (4, 3, 5, 2, 6, 1, 7):
        y_to = lax.rem(y + t, 8)
        push(
            down_hbm.at[pl.ds(pl.multiple_of(reg * 16, 16), 16),
                        pl.ds(pl.multiple_of(y_to * EIGHTH, 128), EIGHTH)],
            wd.at[8 - t, pl.ds(pl.multiple_of(reg * 16, 16), 16), :],
            ws.at[8 - t], wr.at[8 - t], along_y(t),
        )
    x_step(0, 0)
    y_wait(0)
    x_step(0, 1)
    mid_send(0, 0)
    mid_send(0, 1)
    x_step(1, 0)
    weights_wait()
    z_start()
    x_step(1, 1)
    mid_step(0)
    x_step(2, 0)
    z_step(0, 0)
    x_step(2, 1)
    mid_step(1)
    z_step(0, 1)
    loads[0].wait()
    loads[1].wait()
    y_waits(1, 4)
    gate_up(0)
    x_step(3, 0)
    x_step(3, 1)
    mid_step(2)
    z_step(1, 0)
    y_waits(4, 6)
    gate_up(1)
    z_step(1, 1)
    hidden_step(0, 0)
    mid_step(3)
    y_waits(6, 8)
    gate_up(2)
    z_step(2, 0)
    hidden_step(0, 1)
    hidden_step(1, 0)
    z_step(2, 1)
    hidden_step(2, 0)
    hidden_step(0, 2)
    hidden_step(1, 1)
    z_step(3, 0)
    z_step(3, 1)
    hidden_step(2, 1)
    hidden_step(0, 3)
    hidden_step(1, 2)
    loads[2].wait()
    core_wait()
    hidden_step(2, 2)
    down(0, range(8), True)
    part_send(0)
    hidden_step(1, 3)
    down(1, range(8), True)
    part_send(1)
    down(2, (0, 1, 7, 2, 6, 3, 5), True)
    hidden_step(2, 3)
    down(2, (4,), False)
    part_send(2)

    for lane in (0, 1):
        rows[lane] = part_f[64 * lane : 64 * lane + 16, :]
    for d in (1, 7, 2, 6, 3, 5, 4):
        arrive(arrived.at[d], ps.at[d], pr.at[d])
        rows[...] += arrived[d].astype(jnp.float32)
    for lane in (0, 1):
        for j in range(16):
            outgo[lane, j] = rows[lane, j : j + 1, :]
    own = pltpu.make_async_copy(outgo.at[ylo, reg], final.at[ylo, reg], own_sem)
    own.start()
    for swap in (0, 1):
        lane = 1 - ylo if swap else ylo
        for t in range(16):
            if swap or t:
                push(outgo.at[lane, lax.rem(reg + t, 16)], final.at[ylo, reg],
                     fs.at[swap, t], fr.at[swap, t], regroup_peer(swap, t))
    for copy in sends:
        copy.wait_send()
    own.wait()
    for swap in (0, 1):
        lane = 1 - ylo if swap else ylo
        for t in range(16):
            if swap or t:
                arrive(final.at[lane, lax.rem(reg + 16 - t, 16)], fs.at[swap, t], fr.at[swap, t])
    for lane in (0, 1):
        for g in range(16):
            rows[lane, g : g + 1, :] = final[lane, g]
        out_ref[:, lane * EIGHTH : (lane + 1) * EIGHTH] = rows[lane].astype(jnp.bfloat16)


def on_device(tokens, kinds, slots, gains, gate_weight, up_weight, down_weight):
    vmem = pl.BlockSpec(memory_space=pltpu.VMEM)
    hbm = pl.BlockSpec(memory_space=pl.ANY)
    bf16, f32, dma = jnp.bfloat16, jnp.float32, pltpu.SemaphoreType.DMA
    return pl.pallas_call(
        kernel,
        out_shape=pltpu.VMEM((16, D // 4), bf16),
        in_specs=[hbm] * 7,
        out_specs=vmem,
        scratch_shapes=[
            pltpu.VMEM((16, D), bf16),
            pltpu.VMEM((1, 16), jnp.int32),
            pltpu.VMEM((1, 16), jnp.int32),
            pltpu.VMEM((8, D), f32),
            pltpu.VMEM((2, 8, 16, D), bf16),
            pltpu.VMEM((D, UNITS), bf16),
            pltpu.VMEM((D, UNITS), bf16),
            pltpu.VMEM((8, UNITS, EIGHTH), bf16),
            pltpu.VMEM((8, 256, UNITS), bf16),
            pltpu.VMEM((128, UNITS), f32),
            pltpu.VMEM((128, UNITS), f32),
            pltpu.VMEM((256, EIGHTH), f32),
            pltpu.VMEM((2, 8, 16, EIGHTH), bf16),
            pltpu.VMEM((8, 2, 16, EIGHTH), bf16),
            pltpu.VMEM((2, 16, 1, EIGHTH), f32),
            pltpu.VMEM((2, 16, 1, EIGHTH), f32),
            pltpu.VMEM((2, 16, EIGHTH), f32),
            dma((7,)),
            dma((2, 4, 2)), dma((2, 4, 2)),
            dma((2, 4)), dma((2, 4)),
            dma((8, 2)), dma((8, 2)),
            dma((8,)), dma((8,)),
            dma((2, 4, 2)), dma((2, 4, 2)),
            dma((8, 2)), dma((8, 2)),
            dma((3, 2, 4)), dma((3, 2, 4)),
            dma((8,)), dma((8,)),
            dma((2, 16)), dma((2, 16)),
            dma(()),
        ],
        compiler_params=pltpu.CompilerParams(collective_id=0, has_side_effects=True),
    )(tokens, kinds.reshape(1, 16), slots, gains, gate_weight, up_weight, down_weight)


def solution(mesh):
    placed = (
        P(("blk", "regroup"), None),
        P(("blk", "regroup")),
        P(("blk", "regroup"), None),
        P(),
        P(None, ("blk", "hid")),
        P(None, ("blk", "hid")),
        P(("blk", "hid"), None),
    )
    return jax.shard_map(
        on_device,
        mesh=mesh,
        in_specs=placed,
        out_specs=P(("blk", "regroup"), "hid"),
        check_vma=False,
    )
```

```python
import jax
import jax.numpy as jnp
from jax import lax
from jax.experimental import pallas as pl
from jax.experimental.pallas import tpu as pltpu
from jax.sharding import PartitionSpec as P

MESH = pl.DeviceIdType.MESH
epsilon = 1e-05
D = 6144
HALF = D // 2
EIGHTH = D // 8
UNITS = 256
SLOT = {0: 0, 1: 1, 7: 2, 2: 3, 6: 4, 3: 5, 5: 6, 4: 7}
AHEAD = {u: d for d, u in SLOT.items()}
KSTEP = 1536
MID, MID_WIDTH = 2304, 1536
GROUPS = ((0, 4), (4, 6), (6, 8))


def rows_of(group):
    lo, hi = GROUPS[group]
    return 32 * lo, 32 * (hi - lo)


def kernel(
    tokens_hbm, kinds_hbm, slots_hbm, gains_hbm, gate_hbm, up_hbm, down_hbm, out_ref,
    tokens_ref, kinds_ref, slots_ref, gains_ref, panel, wg, wu, wd, hid, acc_g, acc_u, part_f, part, arrived, outgo, final, rows,
    load_sem, xs, xr, ms, mr, ys, yr, ws, wr, zs, zr, cs, cr, hs, hr, ps, pr, fs, fr, own_sem,
):
    blk, reg, hidx = lax.axis_index("blk"), lax.axis_index("regroup"), lax.axis_index("hid")
    x, ylo = lax.div(blk, 2), lax.rem(blk, 2)
    y = hidx * 2 + ylo
    z, core = lax.div(reg, 2), lax.rem(reg, 2)

    def device(x_at, y_at, reg_at):
        return (x_at * 2 + lax.rem(y_at, 2), reg_at, lax.div(y_at, 2))

    def along_x(d):
        return device(lax.rem(x + d, 8), y, reg)

    def along_y(d):
        return device(x, lax.rem(y + d, 8), reg)

    def along_z(d):
        return device(x, y, lax.rem(z + d, 8) * 2 + core)

    partner = device(x, y, z * 2 + 1 - core)
    y_other = hidx * 2 + 1 - ylo

    def regroup_peer(swap, t):
        return device(x, y_other if swap else y, lax.rem(reg + t, 16))

    inputs = [
        pltpu.make_async_copy(tokens_hbm, tokens_ref, load_sem.at[3]),
        pltpu.make_async_copy(gains_hbm, gains_ref, load_sem.at[4]),
        pltpu.make_async_copy(kinds_hbm, kinds_ref, load_sem.at[5]),
        pltpu.make_async_copy(slots_hbm, slots_ref, load_sem.at[6]),
    ]
    for copy in inputs:
        copy.start()

    barrier = pltpu.get_barrier_semaphore()
    peers = [along_y(d) for d in (4, 3, 5, 2, 6, 1, 7)] + [along_x(1), along_x(7)]
    peers += [along_z(1), along_z(7), partner]
    for peer in peers:
        pl.semaphore_signal(barrier, inc=1, device_id=peer, device_id_type=MESH)

    loads = [
        pltpu.make_async_copy(gate_hbm, wg, load_sem.at[0]),
        pltpu.make_async_copy(up_hbm, wu, load_sem.at[1]),
        pltpu.make_async_copy(
            down_hbm.at[:, pl.ds(pl.multiple_of(y * EIGHTH, 128), EIGHTH)], wd.at[0], load_sem.at[2]
        ),
    ]
    for load in loads:
        load.start()
    for copy in inputs:
        copy.wait()

    slot_row = slots_ref[...]
    here = lax.broadcasted_iota(jnp.int32, (16, 16), 0) == jnp.broadcast_to(slot_row, (16, 16))
    placing = jnp.where(here, 1.0, 0.0).astype(jnp.bfloat16)
    kind = jnp.sum(
        jnp.where(here, jnp.broadcast_to(kinds_ref[...], (16, 16)).astype(jnp.float32), 0.0),
        axis=1, keepdims=True,
    )
    values = jnp.dot(placing, tokens_ref[...], preferred_element_type=jnp.float32)
    scale = lax.rsqrt(jnp.mean(values * values, axis=1, keepdims=True) + epsilon)
    gain = jnp.broadcast_to(gains_ref[0:1, :], (16, D))
    for k in range(1, 8):
        gain = jnp.where(kind == float(k), jnp.broadcast_to(gains_ref[k : k + 1, :], (16, D)), gain)
    panel[ylo, 0] = (values * scale * gain).astype(jnp.bfloat16)

    pl.semaphore_wait(barrier, len(peers))
    sends = []

    def push(source, target, send_sem, recv_sem, peer):
        copy = pltpu.make_async_remote_copy(
            src_ref=source, dst_ref=target, send_sem=send_sem, recv_sem=recv_sem,
            device_id=peer, device_id_type=MESH,
        )
        copy.start()
        sends.append(copy)

    def arrive(target, send_sem, recv_sem):
        pltpu.make_async_remote_copy(
            src_ref=target, dst_ref=target, send_sem=send_sem, recv_sem=recv_sem,
            device_id=partner, device_id_type=MESH,
        ).wait_recv()

    def half(lane, d, h):
        return panel.at[lane, SLOT[d % 8], :, pl.ds(h * HALF, HALF)]

    def x_send(step, direction, h):
        d = (-step if direction == 0 else step) % 8
        to = (d - 1 if direction == 0 else d + 1) % 8
        push(half(ylo, d, h), half(ylo, to, h), xs.at[direction, step, h], xr.at[direction, step, h],
             along_x(1 if direction == 0 else 7))

    def x_wait(step, direction, h):
        d = (-step - 1 if direction == 0 else step + 1) % 8
        arrive(half(ylo, d, h), xs.at[direction, step, h], xr.at[direction, step, h])

    def y_part(lane, d, h):
        if d == 0:
            return half(lane, d, h)
        lo, width = (0, MID) if h == 0 else (MID + MID_WIDTH, D - MID - MID_WIDTH)
        return panel.at[lane, SLOT[d], :, pl.ds(lo, width)]

    def y_send(d, h):
        push(y_part(ylo, d, h), y_part(ylo, d, h), ys.at[SLOT[d], h], yr.at[SLOT[d], h],
             along_y(1 if h == 0 else 7))

    def y_wait(u):
        for h in (0, 1):
            arrive(y_part(1 - ylo, AHEAD[u], h), ys.at[u, h], yr.at[u, h])

    def mid(d, step, direction):
        lo, width = (MID, MID_WIDTH) if step < 3 else (MID + direction * (MID_WIDTH // 2), MID_WIDTH // 2)
        return panel.at[1 - ylo, SLOT[d % 8], :, pl.ds(lo, width)]

    def mid_send(step, direction):
        d = -step if direction == 0 else step
        to = d - 1 if direction == 0 else d + 1
        push(mid(d, step, direction), mid(to, step, direction), ms.at[direction, step],
             mr.at[direction, step], along_x(1 if direction == 0 else 7))

    def mid_step(step):
        for direction in (0, 1):
            d = -step - 1 if direction == 0 else step + 1
            arrive(mid(d, step, direction), ms.at[direction, step], mr.at[direction, step])
            if step < 3:
                mid_send(step + 1, direction)

    def x_step(step, h):
        if step < 3:
            for direction in (0, 1):
                x_wait(step, direction, h)
                if step < 2 or h == direction:
                    x_send(step + 1, direction, h)
            for direction in (0, 1):
                y_send((-step - 1 if direction == 0 else step + 1) % 8, h)
        else:
            x_wait(3, h, h)
            y_send(4, h)

    def piece(q, part):
        return wd.at[pl.ds(1, 7), pl.ds(pl.multiple_of(q * 16, 16), 16), pl.ds(part * (EIGHTH // 2), EIGHTH // 2)]

    def z_at(d):
        return lax.rem(z + d + 8, 8) * 2 + core

    def z_send(step, direction, part):
        q = z_at(-step if direction == 0 else step)
        push(piece(q, part), piece(q, part), zs.at[direction, step, part], zr.at[direction, step, part],
             along_z(1 if direction == 0 else 7))

    def core_send(d, part):
        push(piece(z_at(d), part), piece(z_at(d), part), cs.at[d % 8, part], cr.at[d % 8, part], partner)

    def z_start():
        for part in (0, 1):
            for direction in (0, 1):
                z_send(0, direction, part)
        for part in (0, 1):
            core_send(0, part)

    def z_step(step, part):
        for direction in (0, 1) if step < 3 else (part,):
            d = -step - 1 if direction == 0 else step + 1
            arrive(piece(z_at(d), part), zs.at[direction, step, part], zr.at[direction, step, part])
            if step < 2 or (step == 2 and direction == part):
                z_send(step + 1, direction, part)
            core_send(4 if step == 3 else d, part)

    def core_wait():
        for d in range(8):
            q = lax.rem(z + d, 8) * 2 + 1 - core
            for part in (0, 1):
                arrive(piece(q, part), cs.at[d, part], cr.at[d, part])

    def hidden_at(dy, group, step, direction):
        start, count = rows_of(group)
        if step == 3:
            start, count = start + direction * (count // 2), count // 2
        return hid.at[dy % 8, pl.ds(start, count), :]

    def hidden_send(group, step, direction):
        dy = -step if direction == 0 else step
        push(hidden_at(dy, group, step, direction),
             hidden_at(dy - 1 if direction == 0 else dy + 1, group, step, direction),
             hs.at[group, direction, step], hr.at[group, direction, step],
             along_y(1 if direction == 0 else 7))

    def hidden_step(group, step):
        for direction in (0, 1):
            dy = -step - 1 if direction == 0 else step + 1
            arrive(hidden_at(dy, group, step, direction), hs.at[group, direction, step],
                   hr.at[group, direction, step])
            if step < 3:
                hidden_send(group, step + 1, direction)

    def gate_up(group):
        (lo, hi), (start, count) = GROUPS[group], rows_of(group)
        acc_g[0:count, :] = jnp.zeros((count, UNITS), jnp.float32)
        acc_u[0:count, :] = jnp.zeros((count, UNITS), jnp.float32)

        def one(k, carry):
            span = pl.ds(pl.multiple_of(k * KSTEP, KSTEP), KSTEP)
            block = panel[:, lo:hi, :, span].reshape(count, KSTEP)
            acc_g[0:count, :] += jnp.dot(block, wg[span, :], preferred_element_type=jnp.float32)
            acc_u[0:count, :] += jnp.dot(block, wu[span, :], preferred_element_type=jnp.float32)
            return carry

        lax.fori_loop(0, D // KSTEP, one, 0)
        v = acc_g[0:count, :]
        hid[0, start : start + count, :] = (v / (1.0 + jnp.exp(-v)) * acc_u[0:count, :]).astype(jnp.bfloat16)
        for direction in (0, 1):
            hidden_send(group, 0, direction)

    def down(group, pieces, first):
        start, count = rows_of(group)
        for dy in pieces:
            term = jnp.dot(hid[dy, start : start + count, :], wd[dy], preferred_element_type=jnp.float32)
            if first and dy == pieces[0]:
                part_f[start : start + count, :] = term
            else:
                part_f[start : start + count, :] += term

    def part_send(group):
        (lo, hi), (start, count) = GROUPS[group], rows_of(group)
        part[:, lo:hi] = part_f[start : start + count, :].reshape(2, hi - lo, 16, EIGHTH).astype(jnp.bfloat16)
        for u in reversed(range(lo, hi)):
            d = AHEAD[u]
            if d:
                push(part.at[:, u], arrived.at[d], ps.at[d], pr.at[d], along_x(d))

    def weights_wait():
        for t in range(1, 8):
            arrive(wd.at[t, pl.ds(pl.multiple_of(reg * 16, 16), 16), :], ws.at[t], wr.at[t])

    def y_waits(lo, hi):
        for u in range(lo, hi):
            y_wait(u)

    for h in (0, 1):
        for direction in (0, 1):
            x_send(0, direction, h)
        y_send(0, h)
    for t in (4, 3, 5, 2, 6, 1, 7):
        y_to = lax.rem(y + t, 8)
        push(
            down_hbm.at[pl.ds(pl.multiple_of(reg * 16, 16), 16),
                        pl.ds(pl.multiple_of(y_to * EIGHTH, 128), EIGHTH)],
            wd.at[8 - t, pl.ds(pl.multiple_of(reg * 16, 16), 16), :],
            ws.at[8 - t], wr.at[8 - t], along_y(t),
        )
    x_step(0, 0)
    y_wait(0)
    x_step(0, 1)
    mid_send(0, 0)
    mid_send(0, 1)
    x_step(1, 0)
    weights_wait()
    z_start()
    x_step(1, 1)
    mid_step(0)
    x_step(2, 0)
    z_step(0, 0)
    x_step(2, 1)
    mid_step(1)
    z_step(0, 1)
    loads[0].wait()
    loads[1].wait()
    y_waits(1, 4)
    gate_up(0)
    x_step(3, 0)
    x_step(3, 1)
    mid_step(2)
    z_step(1, 0)
    y_waits(4, 6)
    gate_up(1)
    z_step(1, 1)
    hidden_step(0, 0)
    mid_step(3)
    y_waits(6, 8)
    gate_up(2)
    z_step(2, 0)
    hidden_step(0, 1)
    hidden_step(1, 0)
    z_step(2, 1)
    hidden_step(2, 0)
    hidden_step(0, 2)
    hidden_step(1, 1)
    z_step(3, 0)
    z_step(3, 1)
    hidden_step(2, 1)
    hidden_step(0, 3)
    hidden_step(1, 2)
    loads[2].wait()
    core_wait()
    hidden_step(2, 2)
    down(0, range(8), True)
    part_send(0)
    down(2, (0, 1, 7, 2, 6, 3, 5), True)
    hidden_step(1, 3)
    hidden_step(2, 3)
    down(2, (4,), False)
    part_send(2)
    down(1, range(8), True)
    part_send(1)

    for lane in (0, 1):
        rows[lane] = part_f[64 * lane : 64 * lane + 16, :]
    for d in (1, 7, 2, 5, 4, 6, 3):
        arrive(arrived.at[d], ps.at[d], pr.at[d])
        rows[...] += arrived[d].astype(jnp.float32)
    for lane in (0, 1):
        for j in range(16):
            outgo[lane, j] = rows[lane, j : j + 1, :]
    own = pltpu.make_async_copy(outgo.at[ylo, reg], final.at[ylo, reg], own_sem)
    own.start()
    for swap, t in sorted(
        [(swap, t) for swap in (0, 1) for t in range(16) if swap or t],
        key=lambda hop: -(2 * hop[0] + min(hop[1], 16 - hop[1])),
    ):
        lane = 1 - ylo if swap else ylo
        push(outgo.at[lane, lax.rem(reg + t, 16)], final.at[ylo, reg],
             fs.at[swap, t], fr.at[swap, t], regroup_peer(swap, t))
    for copy in sends:
        copy.wait_send()
    own.wait()
    for swap in (0, 1):
        lane = 1 - ylo if swap else ylo
        for t in range(16):
            if swap or t:
                arrive(final.at[lane, lax.rem(reg + 16 - t, 16)], fs.at[swap, t], fr.at[swap, t])
    for lane in (0, 1):
        for g in range(16):
            rows[lane, g : g + 1, :] = final[lane, g]
        out_ref[:, lane * EIGHTH : (lane + 1) * EIGHTH] = rows[lane].astype(jnp.bfloat16)


def on_device(tokens, kinds, slots, gains, gate_weight, up_weight, down_weight):
    vmem = pl.BlockSpec(memory_space=pltpu.VMEM)
    hbm = pl.BlockSpec(memory_space=pl.ANY)
    bf16, f32, dma = jnp.bfloat16, jnp.float32, pltpu.SemaphoreType.DMA
    return pl.pallas_call(
        kernel,
        out_shape=pltpu.VMEM((16, D // 4), bf16),
        in_specs=[hbm] * 7,
        out_specs=vmem,
        scratch_shapes=[
            pltpu.VMEM((16, D), bf16),
            pltpu.VMEM((1, 16), jnp.int32),
            pltpu.VMEM((1, 16), jnp.int32),
            pltpu.VMEM((8, D), f32),
            pltpu.VMEM((2, 8, 16, D), bf16),
            pltpu.VMEM((D, UNITS), bf16),
            pltpu.VMEM((D, UNITS), bf16),
            pltpu.VMEM((8, UNITS, EIGHTH), bf16),
            pltpu.VMEM((8, 256, UNITS), bf16),
            pltpu.VMEM((128, UNITS), f32),
            pltpu.VMEM((128, UNITS), f32),
            pltpu.VMEM((256, EIGHTH), f32),
            pltpu.VMEM((2, 8, 16, EIGHTH), bf16),
            pltpu.VMEM((8, 2, 16, EIGHTH), bf16),
            pltpu.VMEM((2, 16, 1, EIGHTH), f32),
            pltpu.VMEM((2, 16, 1, EIGHTH), f32),
            pltpu.VMEM((2, 16, EIGHTH), f32),
            dma((7,)),
            dma((2, 4, 2)), dma((2, 4, 2)),
            dma((2, 4)), dma((2, 4)),
            dma((8, 2)), dma((8, 2)),
            dma((8,)), dma((8,)),
            dma((2, 4, 2)), dma((2, 4, 2)),
            dma((8, 2)), dma((8, 2)),
            dma((3, 2, 4)), dma((3, 2, 4)),
            dma((8,)), dma((8,)),
            dma((2, 16)), dma((2, 16)),
            dma(()),
        ],
        compiler_params=pltpu.CompilerParams(collective_id=0, has_side_effects=True),
    )(tokens, kinds.reshape(1, 16), slots, gains, gate_weight, up_weight, down_weight)


def solution(mesh):
    placed = (
        P(("blk", "regroup"), None),
        P(("blk", "regroup")),
        P(("blk", "regroup"), None),
        P(),
        P(None, ("blk", "hid")),
        P(None, ("blk", "hid")),
        P(("blk", "hid"), None),
    )
    return jax.shard_map(
        on_device,
        mesh=mesh,
        in_specs=placed,
        out_specs=P(("blk", "regroup"), "hid"),
        check_vma=False,
    )
```
